32 devices in a mesh: gx: 4 (over x, core), gy: 8 (over z, y).
Axes of the slice: x: 2, y: 2, z: 4, core: 2. Of those that a mesh axis runs over, the one named last changes fastest.
Arguments:
- patches: bfloat16 [4096, 1664], P('gy', 'gx'), may hold values from -6 to 6
- segment_ids: int32 [4096], P('gy'), may hold values from 0 to 31, as said below
- image_requests: int32 [32], replicated, may hold values from 0 to 7
- merge_index: int32 [1024, 4], P('gy'), may hold values from 0 to 4095, as said below
- qkv_weight: bfloat16 [1664, 3, 1664], P('gy', None, 'gx'), may hold values from -128 to 128
- out_weight: bfloat16 [1664, 1664], P('gx', 'gy'), may hold values from -0.15625 to 0.15625
- up_weight: bfloat16 [1664, 8192], P('gy', 'gx'), may hold values from -0.15625 to 0.15625
- down_weight: bfloat16 [8192, 1664], P('gx', 'gy'), may hold values from -0.0625 to 0.0625
- merge_weight: bfloat16 [6656, 4096], P('gy', 'gx'), may hold values from -0.078125 to 0.078125
Outputs:
- merged: bfloat16 [1024, 4096], P('gy', 'gx')
- request_norms: float32 [8], replicated
- top_logit: float32 [], replicated
The draws below stay inside these ranges and needn't reach their ends.
Inputs may be any that keep to these rules, and one draw needn't show every extreme that they name: `segment_ids`: segment ids never fall along the tokens; the 512 tokens of block b (tokens b * 512 onward) hold exactly the images b * 4 to (b + 1) * 4 - 1, each a multiple of 4 tokens long. `merge_index`: every token stands in exactly one merged row; the four tokens of merged row m belong to one image, in the block of 512 tokens that holds token 4 * m.
All inputs are finite; a program needn't handle non-finite values.
Results may differ from the reference program's by a relative error of at most 0.011.
Values may be sent and summed in bfloat16 or wider, within the bound.
A program may use at most 128 MiB of HBM per device.

```python
import math
import jax
import jax.numpy as jnp
from jax import lax

D = 1664
HEADS = 16
HEAD = 104
FF = 8192
OUT = 4096
TOK_GRP = 512
IMG_GRP = 4
TOKENS = 4096
IMAGES = 32
REQS = 8
MERGED = 1024


def layout_tables(key):
    layout_key = jax.random.fold_in(key, 11)
    block_count = TOKENS // TOK_GRP
    unit_count = TOK_GRP // 4

    def one_block(block_key):
        cut_key, order_key = jax.random.split(block_key)
        candidates = jax.random.permutation(cut_key, unit_count - 1) + 1
        cut_points = jnp.sort(candidates[:IMG_GRP - 1])
        unit_image = jnp.sum((jnp.arange(unit_count)[:, None] >= cut_points[None, :]).astype(jnp.int32), axis=1)
        token_image = jnp.repeat(unit_image, 4)
        scores = token_image * TOK_GRP + jax.random.permutation(order_key, TOK_GRP)
        ordering = jnp.argsort(scores).astype(jnp.int32)
        return (token_image.astype(jnp.int32), ordering.reshape(unit_count, 4))
    images, orders = jax.vmap(one_block)(jax.random.split(layout_key, block_count))
    block_first = jnp.arange(block_count, dtype=jnp.int32)
    segments = (images + block_first[:, None] * IMG_GRP).reshape(TOKENS)
    groups = (orders + block_first[:, None, None] * TOK_GRP).reshape(MERGED, 4)
    return (segments.astype(jnp.int32), groups.astype(jnp.int32))


def draw_segment_ids(key, part):
    return layout_tables(key)[0]


def draw_merge_index(key, part):
    return layout_tables(key)[1]


def draw_qkv_weight(key, part):
    query_key, noise_key, value_key, order_key = jax.random.split(jax.random.fold_in(key, 5), 4)
    scale = D ** (-0.5)
    query = jax.random.normal(query_key, (D, D), jnp.float32) * scale
    noise = jax.random.normal(noise_key, (D, D), jnp.float32) * scale
    value_part = jax.random.normal(value_key, (D, D), jnp.float32) * scale
    ladder = 2.0 * jnp.power(150.0, jnp.arange(HEADS, dtype=jnp.float32) / (HEADS - 1))
    strength = ladder[jax.random.permutation(order_key, HEADS)]
    column_factor = jnp.repeat(strength, HEAD) / math.sqrt(HEAD)
    key_part = query * column_factor[None, :] + noise
    stacked = jnp.stack([query, key_part, value_part], axis=1)
    return jnp.clip(stacked, -128.0, 128.0).astype(jnp.bfloat16)


def touch_ends(entries, own_key, smallest, largest):
    index_at = [jax.random.randint(jax.random.fold_in(own_key, axis), (), 0, length) for axis, length in enumerate(entries.shape)]
    widest = entries.shape.index(max(entries.shape))
    next_to = index_at[:widest] + [(index_at[widest] + 1) % entries.shape[widest]] + index_at[widest + 1:]
    return entries.at[tuple(index_at)].set(smallest).at[tuple(next_to)].set(largest)


def block_scale(rng, shape, pieces, least, largest):
    def one(dim, shards_of):
        draws = jax.random.uniform(jax.random.fold_in(jax.random.fold_in(rng, 6), dim), (shards_of,), jnp.float32, least / len(pieces), largest / len(pieces))
        return jnp.repeat(jnp.exp(draws), shape[dim] // shards_of).reshape((-1,) + (1,) * (len(shape) - dim - 1))

    loudness = one(*pieces[0])
    for cut in pieces[1:]:
        loudness = loudness * one(*cut)
    return loudness


def normal_values(stream_key, extent, width, most, pieces=(), kind=jnp.bfloat16):
    entries = jax.random.normal(stream_key, extent, jnp.float32) * width
    if len(pieces) > 0:
        entries = block_scale(stream_key, extent, pieces, -0.22, 0.18) * entries
    return jnp.clip(entries, min=-most, max=most).astype(kind)


def setup_inputs(seed: int = 0) -> dict:
    key_of = jax.random.split(jax.random.key(seed), 10)
    patches = normal_values(key_of[0], (TOKENS, D), 1.0, 6.0, ((0, 8), (1, 4)))
    segment_ids = draw_segment_ids(jax.random.fold_in(key_of[9], 71), 0)
    image_requests = touch_ends(jax.random.randint(key_of[2], (IMAGES,), 0, REQS), jax.random.fold_in(key_of[2], 1), 0, REQS - 1).astype(jnp.int32)
    merge_index = draw_merge_index(jax.random.fold_in(key_of[9], 71), 0)
    qkv_weight = draw_qkv_weight(jax.random.fold_in(key_of[9], 71), 0)
    out_weight = normal_values(key_of[5], (D, D), D ** -0.5, 0.15625, ((0, 4), (1, 8)))
    up_weight = normal_values(key_of[6], (D, FF), D ** -0.5, 0.15625, ((0, 8), (1, 4)))
    down_weight = normal_values(key_of[7], (FF, D), FF ** -0.5, 0.0625, ((0, 4), (1, 8)))
    merge_weight = normal_values(key_of[8], (4 * D, OUT), (4 * D) ** -0.5, 0.078125, ((0, 8), (1, 4)))
    return dict(patches=patches, segment_ids=segment_ids, image_requests=image_requests, merge_index=merge_index, qkv_weight=qkv_weight, out_weight=out_weight, up_weight=up_weight, down_weight=down_weight, merge_weight=merge_weight)


def layer_norm(values):
    center = lax.optimization_barrier(jnp.mean(values, axis=-1, keepdims=True))
    square = lax.optimization_barrier(jnp.mean(values * values, axis=-1, keepdims=True))
    return (values - center) * lax.rsqrt(square - center * center + 1e-06)

def attend_block(inputs):
    block_qkv, block_segments = inputs
    queries = block_qkv[:, 0].astype(jnp.float32)
    key_rows = block_qkv[:, 1].astype(jnp.float32)
    value_rows = block_qkv[:, 2].astype(jnp.float32)
    scores = jnp.einsum('qhe,khe->hqk', queries, key_rows) / math.sqrt(HEAD)
    allowed = block_segments[:, None] == block_segments[None, :]
    scores = jnp.where(allowed[None], scores, -1e+30)
    probs = jax.nn.softmax(scores, axis=-1).astype(jnp.bfloat16)
    mixed = jnp.einsum('hqk,khe->qhe', probs.astype(jnp.float32), value_rows)
    return mixed.astype(jnp.bfloat16)

def reference(patches, segment_ids, image_requests, merge_index, qkv_weight, out_weight, up_weight, down_weight, merge_weight):
    stream_in = patches.astype(jnp.float32)
    normed = layer_norm(stream_in).astype(jnp.bfloat16)
    projected = jnp.dot(normed, qkv_weight.reshape(D, 3 * D), preferred_element_type=jnp.float32).astype(jnp.bfloat16)
    block_count = TOKENS // TOK_GRP
    blocked = projected.reshape(block_count, TOK_GRP, 3, HEADS, HEAD)
    mixed = lax.map(attend_block, (blocked, segment_ids.reshape(block_count, TOK_GRP))).reshape(TOKENS, D)
    stream = (stream_in + jnp.dot(mixed, out_weight, preferred_element_type=jnp.float32)).astype(jnp.bfloat16)
    normed_two = layer_norm(stream.astype(jnp.float32)).astype(jnp.bfloat16)
    hidden = jax.nn.gelu(jnp.dot(normed_two, up_weight, preferred_element_type=jnp.float32), approximate=False).astype(jnp.bfloat16)
    final = (stream.astype(jnp.float32) + jnp.dot(hidden, down_weight, preferred_element_type=jnp.float32)).astype(jnp.bfloat16)
    joined = jnp.take(final, merge_index.reshape(-1), axis=0).reshape(MERGED, 4 * D)
    logits = jnp.dot(joined, merge_weight, preferred_element_type=jnp.float32)
    row_squares = lax.optimization_barrier(jnp.sum(jnp.square(final.astype(jnp.float32)), axis=1))
    image_sq = jax.ops.segment_sum(row_squares, segment_ids, num_segments=IMAGES)
    request_sq = jax.ops.segment_sum(image_sq, image_requests, num_segments=REQS)
    return (logits.astype(jnp.bfloat16), jnp.sqrt(request_sq), jnp.max(logits))
```

```python
import math

import jax
import jax.numpy as jnp
import numpy as np
from jax import lax
from jax.experimental import pallas as pl
from jax.experimental.pallas import tpu as pltpu
from jax.sharding import PartitionSpec as P

HEAD = 104
IMG_GRP = 4
MESH = pl.DeviceIdType.MESH


def ring_order(count):
    ny = 2 if count <= 8 else 4
    nz = count // ny
    walk = [z * ny for z in range(nz)]
    for k, z in enumerate(range(nz - 1, -1, -1)):
        ys = range(1, ny) if k % 2 == 0 else range(ny - 1, 0, -1)
        walk += [z * ny + y for y in ys]
    return walk


def layer_norm(values):
    center = jnp.mean(values, axis=-1, keepdims=True)
    square = jnp.mean(values * values, axis=-1, keepdims=True)
    return (values - center) * lax.rsqrt(square - center * center + 1e-06)


def after(value, *others):
    return lax.optimization_barrier((value, *others))[0]


class Ring:
    def __init__(self, count):
        self.count = count
        self.walk = ring_order(count)
        where = np.argsort(np.array(self.walk))
        self.walk_arr = jnp.asarray(np.array(self.walk, np.int32))
        self.here = jnp.asarray(where.astype(np.int32))[lax.axis_index("gy")]
        n = count
        self.right = [(self.walk[i], self.walk[(i + 1) % n]) for i in range(n)]
        self.left = [(self.walk[i], self.walk[(i - 1) % n]) for i in range(n)]

    def origin(self, offset):
        return self.walk_arr[lax.rem(self.here + offset + self.count, self.count)]

    def gather(self, shard, split_axis):
        n = self.count
        found = [(self.origin(0), shard)]
        cw = ccw = shard
        for step in range(1, (n - 1) // 2 + 1):
            cw = lax.ppermute(cw, "gy", self.right)
            ccw = lax.ppermute(ccw, "gy", self.left)
            found.append((self.origin(-step), cw))
            found.append((self.origin(step), ccw))
        half = shard.shape[split_axis] // 2
        first = lax.slice_in_dim(cw, 0, half, axis=split_axis)
        second = lax.slice_in_dim(ccw, half, 2 * half, axis=split_axis)
        first = lax.ppermute(first, "gy", self.right)
        second = lax.ppermute(second, "gy", self.left)
        far = lax.concatenate([first, second], split_axis)
        found.append((self.origin(n // 2), far))
        return found


def pick(stacked, index):
    return lax.dynamic_index_in_dim(stacked, index, 0, keepdims=False)


def sum_chunks(left, found):
    total = None
    for index, shard in found:
        term = jnp.dot(pick(left, index), shard, preferred_element_type=jnp.float32)
        total = term if total is None else total + term
    return total


def chunked(values, count):
    rows, width = values.shape
    return values.reshape(rows, count, width // count).transpose(1, 0, 2)


def place_columns(left, found, count):
    width = found[0][1].shape[0]
    out = jnp.zeros((count, left.shape[0], width), jnp.float32)
    for index, shard in found:
        term = lax.dot_general(
            left, shard, (((1,), (1,)), ((), ())), preferred_element_type=jnp.float32
        )
        out = lax.dynamic_update_index_in_dim(out, term, index, 0)
    return out.transpose(1, 0, 2).reshape(left.shape[0], count * width)


def core_pairs(gx):
    return [(i, i ^ 1) for i in range(gx)]


def x_shift(gx, k):
    return [(i, (i + 2 * k) % gx) for i in range(gx)]


def gather_features(share, gx):
    me = lax.axis_index("gx")
    chip, core = me // 2, me % 2
    chips = gx // 2
    rows, feats = share.shape
    mine = jnp.zeros((chips, rows, feats), share.dtype)
    mine = lax.dynamic_update_index_in_dim(mine, share, chip, 0)
    for k in range(1, chips):
        got = lax.ppermute(share, "gx", x_shift(gx, k))
        mine = lax.dynamic_update_index_in_dim(mine, got, lax.rem(chip - k + chips, chips), 0)
    theirs = lax.ppermute(mine, "gx", core_pairs(gx))
    low = jnp.where(core == 0, mine, theirs)
    high = jnp.where(core == 0, theirs, mine)
    both = jnp.stack([low, high], axis=1)
    return both.transpose(2, 0, 1, 3).reshape(rows, gx * feats)


def add_sum(partial, stream, gx):
    core = lax.axis_index("gx") % 2
    rows = partial.shape[0] // 2
    keep = lax.dynamic_slice_in_dim(partial, core * rows, rows, 0)
    give = lax.dynamic_slice_in_dim(partial, (1 - core) * rows, rows, 0)
    chip_sum = keep + lax.ppermute(give, "gx", core_pairs(gx))
    sent = chip_sum.astype(jnp.bfloat16)
    total = sent.astype(jnp.float32)
    for k in range(1, gx // 2):
        total = total + lax.ppermute(sent, "gx", x_shift(gx, k)).astype(jnp.float32)
    base = lax.dynamic_slice_in_dim(stream, core * rows, rows, 0)
    mine = (base.astype(jnp.float32) + total).astype(jnp.bfloat16)
    theirs = lax.ppermute(mine, "gx", core_pairs(gx))
    low = jnp.where(core == 0, mine, theirs)
    high = jnp.where(core == 0, theirs, mine)
    return jnp.concatenate([low, high], axis=0)


def scalar_kernel(gx, gy, mine_ref, out_ref, slot_a, slot_b, send_a, recv_a, send_b, recv_b):
    mx, my = lax.axis_index("gx"), lax.axis_index("gy")
    barrier = pltpu.get_barrier_semaphore()
    for k in range(1, gx):
        pl.semaphore_signal(
            barrier, inc=1, device_id=(lax.rem(mx + k, gx), my), device_id_type=MESH
        )
    for k in range(1, gy):
        pl.semaphore_signal(
            barrier, inc=1, device_id=(mx, lax.rem(my + k, gy)), device_id_type=MESH
        )
    pl.semaphore_wait(barrier, gx + gy - 2)

    def combine(one, two):
        row = lax.broadcasted_iota(jnp.int32, one.shape, 0)
        return jnp.where(row == 0, jnp.maximum(one, two), one + two)

    copies = []
    for k in range(1, gx):
        copy = pltpu.make_async_remote_copy(
            src_ref=mine_ref,
            dst_ref=slot_a.at[k],
            send_sem=send_a.at[k],
            recv_sem=recv_a.at[k],
            device_id=(lax.rem(mx + k, gx), my),
            device_id_type=MESH,
        )
        copy.start()
        copies.append(copy)
    total = mine_ref[...]
    for k, copy in enumerate(copies):
        copy.wait()
        total = combine(total, slot_a[k + 1])
    slot_b[0] = total
    copies = []
    for k in range(1, gy):
        copy = pltpu.make_async_remote_copy(
            src_ref=slot_b.at[0],
            dst_ref=slot_b.at[k],
            send_sem=send_b.at[k],
            recv_sem=recv_b.at[k],
            device_id=(mx, lax.rem(my + k, gy)),
            device_id_type=MESH,
        )
        copy.start()
        copies.append(copy)
    for k, copy in enumerate(copies):
        copy.wait()
        total = combine(total, slot_b[k + 1])
    out_ref[...] = total


def reduce_scalars(requests, top, gx, gy):
    count = requests.shape[0]
    tile = jnp.zeros((8, 128), jnp.float32)
    tile = tile.at[0, :].set(top).at[1, :count].set(requests)
    out = pl.pallas_call(
        lambda *refs: scalar_kernel(gx, gy, *refs),
        out_shape=jax.ShapeDtypeStruct((8, 128), jnp.float32),
        in_specs=[pl.BlockSpec(memory_space=pltpu.VMEM)],
        out_specs=pl.BlockSpec(memory_space=pltpu.VMEM),
        scratch_shapes=[
            pltpu.VMEM((gx, 8, 128), jnp.float32),
            pltpu.VMEM((gy, 8, 128), jnp.float32),
            pltpu.SemaphoreType.DMA((gx,)),
            pltpu.SemaphoreType.DMA((gx,)),
            pltpu.SemaphoreType.DMA((gy,)),
            pltpu.SemaphoreType.DMA((gy,)),
        ],
        compiler_params=pltpu.CompilerParams(collective_id=0, has_side_effects=True),
        name="scalar_sums",
    )(tile)
    return out[1, :count], out[0, 0]


def attend(projected, segment_ids):
    scores = jnp.einsum(
        "qhe,khe->hqk", projected[:, 0], projected[:, 1], preferred_element_type=jnp.float32
    ) / math.sqrt(HEAD)
    allowed = segment_ids[:, None] == segment_ids[None, :]
    scores = jnp.where(allowed[None], scores, -1e30)
    probs = jax.nn.softmax(scores, axis=-1).astype(jnp.bfloat16)
    mixed = jnp.einsum("hqk,khe->qhe", probs, projected[:, 2], preferred_element_type=jnp.float32)
    return mixed.astype(jnp.bfloat16)


def per_device(
    gx,
    gy,
    patches,
    segment_ids,
    image_requests,
    merge_index,
    qkv_weight,
    out_weight,
    up_weight,
    down_weight,
    merge_weight,
):
    tok_rows, feat_share = patches.shape
    group_index = lax.axis_index("gy")
    own_index = lax.axis_index("gx")
    ring = Ring(gy)
    head_share = qkv_weight.shape[2]
    local_heads = head_share // HEAD

    qkv_found = ring.gather(qkv_weight.reshape(qkv_weight.shape[0], -1), 1)
    out_found = ring.gather(out_weight.T, 1)
    up_found = ring.gather(after(up_weight, qkv_found[-1][1]), 1)
    down_found = ring.gather(after(down_weight.T, out_found[-1][1]), 1)
    half = merge_weight.shape[1] // 2
    merge_a = ring.gather(after(merge_weight[:, :half], up_found[-1][1]), 1)
    merge_b = ring.gather(after(merge_weight[:, half:], down_found[-1][1]), 1)

    stream_full = gather_features(patches, gx)
    normed = layer_norm(stream_full.astype(jnp.float32)).astype(jnp.bfloat16)
    projected = sum_chunks(chunked(normed, gy), qkv_found)
    projected = projected.astype(jnp.bfloat16).reshape(tok_rows, 3, local_heads, HEAD)
    mixed = attend(projected, segment_ids).reshape(tok_rows, head_share)
    head_partial = place_columns(mixed, out_found, gy)
    stream_full = add_sum(head_partial, stream_full, gx)
    normed_two = layer_norm(stream_full.astype(jnp.float32)).astype(jnp.bfloat16)
    hidden = sum_chunks(chunked(normed_two, gy), up_found)
    hidden = jax.nn.gelu(hidden, approximate=False).astype(jnp.bfloat16)
    unit_partial = place_columns(hidden, down_found, gy)
    final_full = add_sum(unit_partial, stream_full, gx)
    final_share = lax.dynamic_slice_in_dim(final_full, own_index * feat_share, feat_share, 1)
    row_squares = jnp.sum(jnp.square(final_share.astype(jnp.float32)), axis=1)
    image_ids = group_index * IMG_GRP + jnp.arange(IMG_GRP, dtype=jnp.int32)
    member = segment_ids[:, None] == image_ids[None, :]
    image_sq = jnp.sum(jnp.where(member, row_squares[:, None], 0.0), axis=0)
    local_requests = lax.dynamic_slice_in_dim(image_requests, group_index * IMG_GRP, IMG_GRP)
    request_count = image_requests.shape[0] // 4
    owner = local_requests[:, None] == jnp.arange(request_count, dtype=jnp.int32)[None, :]
    request_part = jnp.sum(jnp.where(owner, image_sq[:, None], 0.0), axis=0)
    local_index = (merge_index - group_index * tok_rows).reshape(-1)
    joined = jnp.take(final_full, local_index, axis=0).reshape(
        merge_index.shape[0], 4 * final_full.shape[1]
    )
    chunks = chunked(joined, gy)
    logits = jnp.concatenate([sum_chunks(chunks, merge_a), sum_chunks(chunks, merge_b)], axis=1)
    local_top = jnp.max(logits)
    request_sq, top_logit = reduce_scalars(request_part, local_top, gx, gy)
    return (logits.astype(jnp.bfloat16), jnp.sqrt(request_sq), top_logit)


def solution(mesh):
    gx, gy = mesh.shape["gx"], mesh.shape["gy"]
    in_specs = (
        P("gy", "gx"),
        P("gy"),
        P(),
        P("gy", None),
        P("gy", None, "gx"),
        P("gx", "gy"),
        P("gy", "gx"),
        P("gx", "gy"),
        P("gy", "gx"),
    )
    out_specs = (P("gy", "gx"), P(), P())

    def body(*args):
        return per_device(gx, gy, *args)

    return jax.shard_map(
        body, mesh=mesh, in_specs=in_specs, out_specs=out_specs, check_vma=False
    )
```

```python
import math

import jax
import jax.numpy as jnp
import numpy as np
from jax import lax
from jax.experimental import pallas as pl
from jax.experimental.pallas import tpu as pltpu
from jax.sharding import PartitionSpec as P

HEAD = 104
IMG_GRP = 4
MESH = pl.DeviceIdType.MESH


def ring_order(count):
    ny = 2 if count <= 8 else 4
    nz = count // ny
    walk = [z * ny for z in range(nz)]
    for k, z in enumerate(range(nz - 1, -1, -1)):
        ys = range(1, ny) if k % 2 == 0 else range(ny - 1, 0, -1)
        walk += [z * ny + y for y in ys]
    return walk


def layer_norm(values):
    center = jnp.mean(values, axis=-1, keepdims=True)
    square = jnp.mean(values * values, axis=-1, keepdims=True)
    return (values - center) * lax.rsqrt(square - center * center + 1e-06)


def after(value, *others):
    return lax.optimization_barrier((value, *others))[0]


class Ring:
    def __init__(self, count):
        self.count = count
        self.walk = ring_order(count)
        where = np.argsort(np.array(self.walk))
        self.walk_arr = jnp.asarray(np.array(self.walk, np.int32))
        self.here = jnp.asarray(where.astype(np.int32))[lax.axis_index("gy")]
        n = count
        self.right = [(self.walk[i], self.walk[(i + 1) % n]) for i in range(n)]
        self.left = [(self.walk[i], self.walk[(i - 1) % n]) for i in range(n)]

    def origin(self, offset):
        return self.walk_arr[lax.rem(self.here + offset + self.count, self.count)]

    def gather(self, shard, split_axis, use=None):
        n = self.count
        found = [(self.origin(0), shard)]
        cw = ccw = shard
        total = None
        for step in range(1, (n - 1) // 2 + 1):
            if use is not None and step > 1:
                for index, block in found[max(0, 2 * step - 5) : 2 * step - 3]:
                    total = use(total, index, block)
                cw, ccw, total = lax.optimization_barrier((cw, ccw, total))
            cw = lax.ppermute(cw, "gy", self.right)
            ccw = lax.ppermute(ccw, "gy", self.left)
            found.append((self.origin(-step), cw))
            found.append((self.origin(step), ccw))
        half = shard.shape[split_axis] // 2
        first = lax.slice_in_dim(cw, 0, half, axis=split_axis)
        second = lax.slice_in_dim(ccw, half, 2 * half, axis=split_axis)
        first = lax.ppermute(first, "gy", self.right)
        second = lax.ppermute(second, "gy", self.left)
        far = lax.concatenate([first, second], split_axis)
        found.append((self.origin(n // 2), far))
        if use is None:
            return found
        for index, block in found[max(0, 2 * ((n - 1) // 2) - 3) :]:
            total = use(total, index, block)
        return total


def pick(stacked, index):
    return lax.dynamic_index_in_dim(stacked, index, 0, keepdims=False)


def sum_chunks(left, found):
    total = None
    for index, shard in found:
        total = add_chunk(left, total, index, shard)
    return total


def add_chunk(left, total, index, shard):
    term = jnp.dot(pick(left, index), shard, preferred_element_type=jnp.float32)
    return term if total is None else total + term


def chunked(values, count):
    rows, width = values.shape
    return values.reshape(rows, count, width // count).transpose(1, 0, 2)


def place_columns(left, found, count):
    width = found[0][1].shape[0]
    out = jnp.zeros((count, left.shape[0], width), jnp.float32)
    for index, shard in found:
        term = lax.dot_general(
            left, shard, (((1,), (1,)), ((), ())), preferred_element_type=jnp.float32
        )
        out = lax.dynamic_update_index_in_dim(out, term, index, 0)
    return out.transpose(1, 0, 2).reshape(left.shape[0], count * width)


def core_pairs(gx):
    return [(i, i ^ 1) for i in range(gx)]


def x_shift(gx, k):
    return [(i, (i + 2 * k) % gx) for i in range(gx)]


def gather_features(share, gx):
    me = lax.axis_index("gx")
    chip, core = me // 2, me % 2
    chips = gx // 2
    rows, feats = share.shape
    mine = jnp.zeros((chips, rows, feats), share.dtype)
    mine = lax.dynamic_update_index_in_dim(mine, share, chip, 0)
    for k in range(1, chips):
        got = lax.ppermute(share, "gx", x_shift(gx, k))
        mine = lax.dynamic_update_index_in_dim(mine, got, lax.rem(chip - k + chips, chips), 0)
    theirs = lax.ppermute(mine, "gx", core_pairs(gx))
    low = jnp.where(core == 0, mine, theirs)
    high = jnp.where(core == 0, theirs, mine)
    both = jnp.stack([low, high], axis=1)
    return both.transpose(2, 0, 1, 3).reshape(rows, gx * feats)


def add_sum(partial, stream, gx):
    core = lax.axis_index("gx") % 2
    rows = partial.shape[0] // 2
    keep = lax.dynamic_slice_in_dim(partial, core * rows, rows, 0)
    give = lax.dynamic_slice_in_dim(partial, (1 - core) * rows, rows, 0)
    chip_sum = keep + lax.ppermute(give, "gx", core_pairs(gx))
    sent = chip_sum.astype(jnp.bfloat16)
    total = sent.astype(jnp.float32)
    for k in range(1, gx // 2):
        total = total + lax.ppermute(sent, "gx", x_shift(gx, k)).astype(jnp.float32)
    base = lax.dynamic_slice_in_dim(stream, core * rows, rows, 0)
    mine = (base.astype(jnp.float32) + total).astype(jnp.bfloat16)
    theirs = lax.ppermute(mine, "gx", core_pairs(gx))
    low = jnp.where(core == 0, mine, theirs)
    high = jnp.where(core == 0, theirs, mine)
    return jnp.concatenate([low, high], axis=0)


def scalar_kernel(gx, gy, mine_ref, out_ref, slot_a, slot_b, send_a, recv_a, send_b, recv_b):
    mx, my = lax.axis_index("gx"), lax.axis_index("gy")
    barrier = pltpu.get_barrier_semaphore()
    for k in range(1, gx):
        pl.semaphore_signal(
            barrier, inc=1, device_id=(lax.rem(mx + k, gx), my), device_id_type=MESH
        )
    for k in range(1, gy):
        pl.semaphore_signal(
            barrier, inc=1, device_id=(mx, lax.rem(my + k, gy)), device_id_type=MESH
        )
    pl.semaphore_wait(barrier, gx + gy - 2)

    def combine(one, two):
        row = lax.broadcasted_iota(jnp.int32, one.shape, 0)
        return jnp.where(row == 0, jnp.maximum(one, two), one + two)

    copies = []
    for k in range(1, gx):
        copy = pltpu.make_async_remote_copy(
            src_ref=mine_ref,
            dst_ref=slot_a.at[k],
            send_sem=send_a.at[k],
            recv_sem=recv_a.at[k],
            device_id=(lax.rem(mx + k, gx), my),
            device_id_type=MESH,
        )
        copy.start()
        copies.append(copy)
    total = mine_ref[...]
    for k, copy in enumerate(copies):
        copy.wait()
        total = combine(total, slot_a[k + 1])
    slot_b[0] = total
    copies = []
    for k in range(1, gy):
        copy = pltpu.make_async_remote_copy(
            src_ref=slot_b.at[0],
            dst_ref=slot_b.at[k],
            send_sem=send_b.at[k],
            recv_sem=recv_b.at[k],
            device_id=(mx, lax.rem(my + k, gy)),
            device_id_type=MESH,
        )
        copy.start()
        copies.append(copy)
    for k, copy in enumerate(copies):
        copy.wait()
        total = combine(total, slot_b[k + 1])
    out_ref[...] = total


def reduce_scalars(requests, top, gx, gy):
    count = requests.shape[0]
    tile = jnp.zeros((8, 128), jnp.float32)
    tile = tile.at[0, :].set(top).at[1, :count].set(requests)
    out = pl.pallas_call(
        lambda *refs: scalar_kernel(gx, gy, *refs),
        out_shape=jax.ShapeDtypeStruct((8, 128), jnp.float32),
        in_specs=[pl.BlockSpec(memory_space=pltpu.VMEM)],
        out_specs=pl.BlockSpec(memory_space=pltpu.VMEM),
        scratch_shapes=[
            pltpu.VMEM((gx, 8, 128), jnp.float32),
            pltpu.VMEM((gy, 8, 128), jnp.float32),
            pltpu.SemaphoreType.DMA((gx,)),
            pltpu.SemaphoreType.DMA((gx,)),
            pltpu.SemaphoreType.DMA((gy,)),
            pltpu.SemaphoreType.DMA((gy,)),
        ],
        compiler_params=pltpu.CompilerParams(collective_id=0, has_side_effects=True),
        name="scalar_sums",
    )(tile)
    return out[1, :count], out[0, 0]


def attend(projected, segment_ids):
    scores = jnp.einsum(
        "qhe,khe->hqk", projected[:, 0], projected[:, 1], preferred_element_type=jnp.float32
    ) / math.sqrt(HEAD)
    allowed = segment_ids[:, None] == segment_ids[None, :]
    scores = jnp.where(allowed[None], scores, -1e30)
    probs = jax.nn.softmax(scores, axis=-1).astype(jnp.bfloat16)
    mixed = jnp.einsum("hqk,khe->qhe", probs, projected[:, 2], preferred_element_type=jnp.float32)
    return mixed.astype(jnp.bfloat16)


def per_device(
    gx,
    gy,
    patches,
    segment_ids,
    image_requests,
    merge_index,
    qkv_weight,
    out_weight,
    up_weight,
    down_weight,
    merge_weight,
):
    tok_rows, feat_share = patches.shape
    group_index = lax.axis_index("gy")
    own_index = lax.axis_index("gx")
    ring = Ring(gy)
    head_share = qkv_weight.shape[2]
    local_heads = head_share // HEAD

    qkv_found = ring.gather(qkv_weight.reshape(qkv_weight.shape[0], -1), 1)
    out_found = ring.gather(out_weight.T, 1)
    down_found = ring.gather(after(down_weight.T, out_found[-1][1]), 1)
    merge_full = lax.all_gather(merge_weight, "gy", axis=0, tiled=True)

    stream_full = gather_features(patches, gx)
    normed = layer_norm(stream_full.astype(jnp.float32)).astype(jnp.bfloat16)
    projected = sum_chunks(chunked(normed, gy), qkv_found)
    projected = projected.astype(jnp.bfloat16).reshape(tok_rows, 3, local_heads, HEAD)
    mixed = attend(projected, segment_ids).reshape(tok_rows, head_share)
    head_partial = place_columns(mixed, out_found, gy)
    stream_full = add_sum(head_partial, stream_full, gx)
    normed_two = layer_norm(stream_full.astype(jnp.float32)).astype(jnp.bfloat16)
    left = chunked(normed_two, gy)

    def use(total, index, block):
        return add_chunk(left, total, index, block)

    hidden = ring.gather(after(up_weight, qkv_found[-1][1]), 1, use)
    hidden = jax.nn.gelu(hidden, approximate=False).astype(jnp.bfloat16)
    unit_partial = place_columns(hidden, down_found, gy)
    final_full = add_sum(unit_partial, stream_full, gx)
    final_share = lax.dynamic_slice_in_dim(final_full, own_index * feat_share, feat_share, 1)
    row_squares = jnp.sum(jnp.square(final_share.astype(jnp.float32)), axis=1)
    image_ids = group_index * IMG_GRP + jnp.arange(IMG_GRP, dtype=jnp.int32)
    member = segment_ids[:, None] == image_ids[None, :]
    image_sq = jnp.sum(jnp.where(member, row_squares[:, None], 0.0), axis=0)
    local_requests = lax.dynamic_slice_in_dim(image_requests, group_index * IMG_GRP, IMG_GRP)
    request_count = image_requests.shape[0] // 4
    owner = local_requests[:, None] == jnp.arange(request_count, dtype=jnp.int32)[None, :]
    request_part = jnp.sum(jnp.where(owner, image_sq[:, None], 0.0), axis=0)
    local_index = (merge_index - group_index * tok_rows).reshape(-1)
    joined = jnp.take(final_full, local_index, axis=0).reshape(
        merge_index.shape[0], 4 * final_full.shape[1]
    )
    logits = jnp.dot(joined, merge_full, preferred_element_type=jnp.float32)
    local_top = jnp.max(logits)
    request_sq, top_logit = reduce_scalars(request_part, local_top, gx, gy)
    return (logits.astype(jnp.bfloat16), jnp.sqrt(request_sq), top_logit)


def solution(mesh):
    gx, gy = mesh.shape["gx"], mesh.shape["gy"]
    in_specs = (
        P("gy", "gx"),
        P("gy"),
        P(),
        P("gy", None),
        P("gy", None, "gx"),
        P("gx", "gy"),
        P("gy", "gx"),
        P("gx", "gy"),
        P("gy", "gx"),
    )
    out_specs = (P("gy", "gx"), P(), P())

    def body(*args):
        return per_device(gx, gy, *args)

    return jax.shard_map(
        body, mesh=mesh, in_specs=in_specs, out_specs=out_specs, check_vma=False
    )
```

```python
import math

import jax
import jax.numpy as jnp
import numpy as np
from jax import lax
from jax.experimental import pallas as pl
from jax.experimental.pallas import tpu as pltpu
from jax.sharding import PartitionSpec as P

HEAD = 104
IMG_GRP = 4
MESH = pl.DeviceIdType.MESH


def ring_order(count):
    ny = 2 if count <= 8 else 4
    nz = count // ny
    walk = [z * ny for z in range(nz)]
    for k, z in enumerate(range(nz - 1, -1, -1)):
        ys = range(1, ny) if k % 2 == 0 else range(ny - 1, 0, -1)
        walk += [z * ny + y for y in ys]
    return walk


def layer_norm(values):
    center = jnp.mean(values, axis=-1, keepdims=True)
    square = jnp.mean(values * values, axis=-1, keepdims=True)
    return (values - center) * lax.rsqrt(square - center * center + 1e-06)


def after(value, *others):
    return lax.optimization_barrier((value, *others))[0]


class Ring:
    def __init__(self, count):
        self.count = n = count
        walk = ring_order(count)
        where = np.argsort(np.array(walk))
        table = np.array([[walk[(where[g] + k) % n] for k in range(n)] for g in range(n)])
        row = lax.axis_index("gy").astype(jnp.uint32)
        row = lax.dynamic_slice(
            jnp.asarray(table.astype(np.uint32)), (row, jnp.uint32(0)), (1, n)
        )
        self.origins = [lax.reshape(lax.slice(row, (0, k), (1, k + 1)), ()) for k in range(n)]
        self.right = [(walk[i], walk[(i + 1) % n]) for i in range(n)]
        self.left = [(walk[i], walk[(i - 1) % n]) for i in range(n)]

    def origin(self, offset):
        return self.origins[offset % self.count]

    def gather(self, shard, split_axis):
        n = self.count
        found = [(self.origin(0), shard)]
        cw = ccw = shard
        for step in range(1, (n - 1) // 2 + 1):
            cw = lax.ppermute(cw, "gy", self.right)
            ccw = lax.ppermute(ccw, "gy", self.left)
            found.append((self.origin(-step), cw))
            found.append((self.origin(step), ccw))
        half = shard.shape[split_axis] // 2
        first = lax.slice_in_dim(cw, 0, half, axis=split_axis)
        second = lax.slice_in_dim(ccw, half, 2 * half, axis=split_axis)
        first = lax.ppermute(first, "gy", self.right)
        second = lax.ppermute(second, "gy", self.left)
        far = lax.concatenate([first, second], split_axis)
        found.append((self.origin(n // 2), far))
        return found


def step_of(found, step):
    return [found[2 * step - 1][1], found[2 * step][1]]


def pick(stacked, index):
    zero = jnp.uint32(0)
    return lax.dynamic_slice(stacked, (index, zero, zero), (1,) + stacked.shape[1:])[0]


def sum_chunks(left, found):
    total = None
    for index, shard in found:
        total = add_chunk(left, total, index, shard)
    return total


def add_chunk(left, total, index, shard):
    term = jnp.dot(pick(left, index), shard, preferred_element_type=jnp.float32)
    return term if total is None else total + term


def chunked(values, count):
    rows, width = values.shape
    return values.reshape(rows, count, width // count).transpose(1, 0, 2)


def place_columns(left, found, count):
    width = found[0][1].shape[0]
    out = jnp.zeros((count, left.shape[0], width), jnp.float32)
    for index, shard in found:
        term = lax.dot_general(
            left, shard, (((1,), (1,)), ((), ())), preferred_element_type=jnp.float32
        )
        out = lax.dynamic_update_slice(out, term[None], (index, jnp.uint32(0), jnp.uint32(0)))
    return out.transpose(1, 0, 2).reshape(left.shape[0], count * width)


def core_pairs(gx):
    return [(i, i ^ 1) for i in range(gx)]


def x_shift(gx, k):
    return [(i, (i + 2 * k) % gx) for i in range(gx)]


def gather_features(share, gx):
    me = lax.axis_index("gx")
    chip, core = me // 2, me % 2
    chips = gx // 2
    rows, feats = share.shape
    mine = jnp.zeros((chips, rows, feats), share.dtype)
    mine = lax.dynamic_update_index_in_dim(mine, share, chip, 0)
    for k in range(1, chips):
        got = lax.ppermute(share, "gx", x_shift(gx, k))
        mine = lax.dynamic_update_index_in_dim(mine, got, lax.rem(chip - k + chips, chips), 0)
    theirs = lax.ppermute(mine, "gx", core_pairs(gx))
    low = jnp.where(core == 0, mine, theirs)
    high = jnp.where(core == 0, theirs, mine)
    both = jnp.stack([low, high], axis=1)
    return both.transpose(2, 0, 1, 3).reshape(rows, gx * feats)


def add_sum(partial, stream, gx):
    core = lax.axis_index("gx") % 2
    rows = partial.shape[0] // 2
    keep = lax.dynamic_slice_in_dim(partial, core * rows, rows, 0)
    give = lax.dynamic_slice_in_dim(partial, (1 - core) * rows, rows, 0)
    chip_sum = keep + lax.ppermute(give, "gx", core_pairs(gx))
    sent = chip_sum.astype(jnp.bfloat16)
    total = sent.astype(jnp.float32)
    for k in range(1, gx // 2):
        total = total + lax.ppermute(sent, "gx", x_shift(gx, k)).astype(jnp.float32)
    base = lax.dynamic_slice_in_dim(stream, core * rows, rows, 0)
    mine = (base.astype(jnp.float32) + total).astype(jnp.bfloat16)
    theirs = lax.ppermute(mine, "gx", core_pairs(gx))
    low = jnp.where(core == 0, mine, theirs)
    high = jnp.where(core == 0, theirs, mine)
    return jnp.concatenate([low, high], axis=0)


def scalar_kernel(gx, gy, mine_ref, out_ref, slot_a, slot_b, send_a, recv_a, send_b, recv_b):
    mx, my = lax.axis_index("gx"), lax.axis_index("gy")
    barrier = pltpu.get_barrier_semaphore()
    for k in range(1, gx):
        pl.semaphore_signal(
            barrier, inc=1, device_id=(lax.rem(mx + k, gx), my), device_id_type=MESH
        )
    for k in range(1, gy):
        pl.semaphore_signal(
            barrier, inc=1, device_id=(mx, lax.rem(my + k, gy)), device_id_type=MESH
        )
    pl.semaphore_wait(barrier, gx + gy - 2)

    def combine(one, two):
        row = lax.broadcasted_iota(jnp.int32, one.shape, 0)
        return jnp.where(row == 0, jnp.maximum(one, two), one + two)

    copies = []
    for k in range(1, gx):
        copy = pltpu.make_async_remote_copy(
            src_ref=mine_ref,
            dst_ref=slot_a.at[k],
            send_sem=send_a.at[k],
            recv_sem=recv_a.at[k],
            device_id=(lax.rem(mx + k, gx), my),
            device_id_type=MESH,
        )
        copy.start()
        copies.append(copy)
    total = mine_ref[...]
    for k, copy in enumerate(copies):
        copy.wait()
        total = combine(total, slot_a[k + 1])
    slot_b[0] = total
    copies = []
    for k in range(1, gy):
        copy = pltpu.make_async_remote_copy(
            src_ref=slot_b.at[0],
            dst_ref=slot_b.at[k],
            send_sem=send_b.at[k],
            recv_sem=recv_b.at[k],
            device_id=(mx, lax.rem(my + k, gy)),
            device_id_type=MESH,
        )
        copy.start()
        copies.append(copy)
    for k, copy in enumerate(copies):
        copy.wait()
        total = combine(total, slot_b[k + 1])
    out_ref[...] = total


def reduce_scalars(requests, top, gx, gy):
    count = requests.shape[0]
    tile = jnp.zeros((8, 128), jnp.float32)
    tile = tile.at[0, :].set(top).at[1, :count].set(requests)
    out = pl.pallas_call(
        lambda *refs: scalar_kernel(gx, gy, *refs),
        out_shape=jax.ShapeDtypeStruct((8, 128), jnp.float32),
        in_specs=[pl.BlockSpec(memory_space=pltpu.VMEM)],
        out_specs=pl.BlockSpec(memory_space=pltpu.VMEM),
        scratch_shapes=[
            pltpu.VMEM((gx, 8, 128), jnp.float32),
            pltpu.VMEM((gy, 8, 128), jnp.float32),
            pltpu.SemaphoreType.DMA((gx,)),
            pltpu.SemaphoreType.DMA((gx,)),
            pltpu.SemaphoreType.DMA((gy,)),
            pltpu.SemaphoreType.DMA((gy,)),
        ],
        compiler_params=pltpu.CompilerParams(collective_id=0, has_side_effects=True),
        name="scalar_sums",
    )(tile)
    return out[1, :count], out[0, 0]


def attend(projected, segment_ids):
    scores = jnp.einsum(
        "qhe,khe->hqk", projected[:, 0], projected[:, 1], preferred_element_type=jnp.float32
    ) / math.sqrt(HEAD)
    allowed = segment_ids[:, None] == segment_ids[None, :]
    scores = jnp.where(allowed[None], scores, -1e30)
    probs = jax.nn.softmax(scores, axis=-1).astype(jnp.bfloat16)
    mixed = jnp.einsum("hqk,khe->qhe", probs, projected[:, 2], preferred_element_type=jnp.float32)
    return mixed.astype(jnp.bfloat16)


def per_device(
    gx,
    gy,
    patches,
    segment_ids,
    image_requests,
    merge_index,
    qkv_weight,
    out_weight,
    up_weight,
    down_weight,
    merge_weight,
):
    tok_rows, feat_share = patches.shape
    group_index = lax.axis_index("gy")
    own_index = lax.axis_index("gx")
    ring = Ring(gy)
    head_share = qkv_weight.shape[2]
    local_heads = head_share // HEAD

    qkv_found = ring.gather(qkv_weight.reshape(qkv_weight.shape[0], -1), 1)
    out_found = ring.gather(out_weight.T, 1)
    up_found = ring.gather(up_weight, 1)
    down_found = ring.gather(down_weight.T, 1)
    first_steps = step_of(up_found, 1) + step_of(down_found, 1)
    second_steps = step_of(up_found, 2) + step_of(down_found, 2)
    merge_full = lax.all_gather(after(merge_weight, *second_steps), "gy", axis=0, tiled=True)

    stream_full = gather_features(patches, gx)
    normed = layer_norm(stream_full.astype(jnp.float32)).astype(jnp.bfloat16)
    projected = sum_chunks(chunked(normed, gy), qkv_found)
    projected = after(projected.astype(jnp.bfloat16), *first_steps).reshape(tok_rows, 3, local_heads, HEAD)
    mixed = attend(projected, segment_ids).reshape(tok_rows, head_share)
    head_partial = place_columns(mixed, out_found, gy)
    stream_full = add_sum(head_partial, stream_full, gx)
    stream_full = after(stream_full, *second_steps)
    normed_two = layer_norm(stream_full.astype(jnp.float32)).astype(jnp.bfloat16)
    hidden = sum_chunks(chunked(normed_two, gy), up_found)
    hidden = jax.nn.gelu(hidden, approximate=False).astype(jnp.bfloat16)
    unit_partial = place_columns(hidden, down_found, gy)
    final_full = add_sum(unit_partial, stream_full, gx)
    final_share = lax.dynamic_slice_in_dim(final_full, own_index * feat_share, feat_share, 1)
    row_squares = jnp.sum(jnp.square(final_share.astype(jnp.float32)), axis=1)
    image_ids = group_index * IMG_GRP + jnp.arange(IMG_GRP, dtype=jnp.int32)
    member = segment_ids[:, None] == image_ids[None, :]
    image_sq = jnp.sum(jnp.where(member, row_squares[:, None], 0.0), axis=0)
    local_requests = lax.dynamic_slice_in_dim(image_requests, group_index * IMG_GRP, IMG_GRP)
    request_count = image_requests.shape[0] // 4
    owner = local_requests[:, None] == jnp.arange(request_count, dtype=jnp.int32)[None, :]
    request_part = jnp.sum(jnp.where(owner, image_sq[:, None], 0.0), axis=0)
    local_index = (merge_index - group_index * tok_rows).reshape(-1)
    joined = jnp.take(final_full, local_index, axis=0).reshape(
        merge_index.shape[0], 4 * final_full.shape[1]
    )
    logits = jnp.dot(joined, merge_full, preferred_element_type=jnp.float32)
    local_top = jnp.max(logits)
    request_sq, top_logit = reduce_scalars(request_part, local_top, gx, gy)
    return (logits.astype(jnp.bfloat16), jnp.sqrt(request_sq), top_logit)


def solution(mesh):
    gx, gy = mesh.shape["gx"], mesh.shape["gy"]
    in_specs = (
        P("gy", "gx"),
        P("gy"),
        P(),
        P("gy", None),
        P("gy", None, "gx"),
        P("gx", "gy"),
        P("gy", "gx"),
        P("gx", "gy"),
        P("gy", "gx"),
    )
    out_specs = (P("gy", "gx"), P(), P())

    def body(*args):
        return per_device(gx, gy, *args)

    return jax.shard_map(
        body, mesh=mesh, in_specs=in_specs, out_specs=out_specs, check_vma=False
    )
```

```python
import math

import jax
import jax.numpy as jnp
import numpy as np
from jax import lax
from jax.experimental import pallas as pl
from jax.experimental.pallas import tpu as pltpu
from jax.sharding import PartitionSpec as P

HEAD = 104
IMG_GRP = 4
MESH = pl.DeviceIdType.MESH


def ring_order(count):
    ny = 2 if count <= 8 else 4
    nz = count // ny
    walk = [z * ny for z in range(nz)]
    for k, z in enumerate(range(nz - 1, -1, -1)):
        ys = range(1, ny) if k % 2 == 0 else range(ny - 1, 0, -1)
        walk += [z * ny + y for y in ys]
    return walk


def layer_norm(values):
    center = jnp.mean(values, axis=-1, keepdims=True)
    square = jnp.mean(values * values, axis=-1, keepdims=True)
    return (values - center) * lax.rsqrt(square - center * center + 1e-06)


def after(value, *others):
    return lax.optimization_barrier((value, *others))[0]


class Ring:
    def __init__(self, count):
        self.count = n = count
        walk = ring_order(count)
        where = np.argsort(np.array(walk))
        table = np.array([[walk[(where[g] + k) % n] for k in range(n)] for g in range(n)])
        row = lax.axis_index("gy").astype(jnp.uint32)
        row = lax.dynamic_slice(
            jnp.asarray(table.astype(np.uint32)), (row, jnp.uint32(0)), (1, n)
        )
        self.origins = [lax.reshape(lax.slice(row, (0, k), (1, k + 1)), ()) for k in range(n)]
        self.right = [(walk[i], walk[(i + 1) % n]) for i in range(n)]
        self.left = [(walk[i], walk[(i - 1) % n]) for i in range(n)]

    def origin(self, offset):
        return self.origins[offset % self.count]

    def steps(self, shard):
        found = [(self.origin(0), shard)]
        cw = ccw = shard
        for step in range(1, (self.count - 1) // 2 + 1):
            cw = lax.ppermute(cw, "gy", self.right)
            ccw = lax.ppermute(ccw, "gy", self.left)
            found.append((self.origin(-step), cw))
            found.append((self.origin(step), ccw))
        return found

    def last(self, cw, ccw, split_axis):
        half = cw.shape[split_axis] // 2
        first = lax.slice_in_dim(cw, 0, half, axis=split_axis)
        second = lax.slice_in_dim(ccw, half, 2 * half, axis=split_axis)
        first = lax.ppermute(first, "gy", self.right)
        second = lax.ppermute(second, "gy", self.left)
        return (self.origin(self.count // 2), lax.concatenate([first, second], split_axis))

    def gather(self, shard, split_axis):
        found = self.steps(shard)
        return found + [self.last(found[-2][1], found[-1][1], split_axis)]


def step_of(found, step):
    return [found[2 * step - 1][1], found[2 * step][1]]


def pick(stacked, index):
    zero = jnp.uint32(0)
    return lax.dynamic_slice(stacked, (index, zero, zero), (1,) + stacked.shape[1:])[0]


def sum_chunks(left, found):
    total = None
    for index, shard in found:
        total = add_chunk(left, total, index, shard)
    return total


def add_chunk(left, total, index, shard):
    term = jnp.dot(pick(left, index), shard, preferred_element_type=jnp.float32)
    return term if total is None else total + term


def chunked(values, count):
    rows, width = values.shape
    return values.reshape(rows, count, width // count).transpose(1, 0, 2)


def place_columns(left, found, count):
    width = found[0][1].shape[0]
    out = jnp.zeros((count, left.shape[0], width), jnp.float32)
    for index, shard in found:
        term = lax.dot_general(
            left, shard, (((1,), (1,)), ((), ())), preferred_element_type=jnp.float32
        )
        out = lax.dynamic_update_slice(out, term[None], (index, jnp.uint32(0), jnp.uint32(0)))
    return out.transpose(1, 0, 2).reshape(left.shape[0], count * width)


def core_pairs(gx):
    return [(i, i ^ 1) for i in range(gx)]


def x_shift(gx, k):
    return [(i, (i + 2 * k) % gx) for i in range(gx)]


def gather_features(share, gx):
    me = lax.axis_index("gx")
    chip, core = me // 2, me % 2
    chips = gx // 2
    rows, feats = share.shape
    mine = jnp.zeros((chips, rows, feats), share.dtype)
    mine = lax.dynamic_update_index_in_dim(mine, share, chip, 0)
    for k in range(1, chips):
        got = lax.ppermute(share, "gx", x_shift(gx, k))
        mine = lax.dynamic_update_index_in_dim(mine, got, lax.rem(chip - k + chips, chips), 0)
    theirs = lax.ppermute(mine, "gx", core_pairs(gx))
    low = jnp.where(core == 0, mine, theirs)
    high = jnp.where(core == 0, theirs, mine)
    both = jnp.stack([low, high], axis=1)
    return both.transpose(2, 0, 1, 3).reshape(rows, gx * feats)


def add_sum(partial, stream, gx):
    core = lax.axis_index("gx") % 2
    rows = partial.shape[0] // 2
    keep = lax.dynamic_slice_in_dim(partial, core * rows, rows, 0)
    give = lax.dynamic_slice_in_dim(partial, (1 - core) * rows, rows, 0)
    chip_sum = keep + lax.ppermute(give, "gx", core_pairs(gx))
    sent = chip_sum.astype(jnp.bfloat16)
    total = sent.astype(jnp.float32)
    for k in range(1, gx // 2):
        total = total + lax.ppermute(sent, "gx", x_shift(gx, k)).astype(jnp.float32)
    base = lax.dynamic_slice_in_dim(stream, core * rows, rows, 0)
    mine = (base.astype(jnp.float32) + total).astype(jnp.bfloat16)
    theirs = lax.ppermute(mine, "gx", core_pairs(gx))
    low = jnp.where(core == 0, mine, theirs)
    high = jnp.where(core == 0, theirs, mine)
    return jnp.concatenate([low, high], axis=0)


def scalar_kernel(gx, gy, mine_ref, out_ref, slot_a, slot_b, send_a, recv_a, send_b, recv_b):
    mx, my = lax.axis_index("gx"), lax.axis_index("gy")
    barrier = pltpu.get_barrier_semaphore()
    for k in range(1, gx):
        pl.semaphore_signal(
            barrier, inc=1, device_id=(lax.rem(mx + k, gx), my), device_id_type=MESH
        )
    for k in range(1, gy):
        pl.semaphore_signal(
            barrier, inc=1, device_id=(mx, lax.rem(my + k, gy)), device_id_type=MESH
        )
    pl.semaphore_wait(barrier, gx + gy - 2)

    def combine(one, two):
        row = lax.broadcasted_iota(jnp.int32, one.shape, 0)
        return jnp.where(row == 0, jnp.maximum(one, two), one + two)

    copies = []
    for k in range(1, gx):
        copy = pltpu.make_async_remote_copy(
            src_ref=mine_ref,
            dst_ref=slot_a.at[k],
            send_sem=send_a.at[k],
            recv_sem=recv_a.at[k],
            device_id=(lax.rem(mx + k, gx), my),
            device_id_type=MESH,
        )
        copy.start()
        copies.append(copy)
    total = mine_ref[...]
    for k, copy in enumerate(copies):
        copy.wait()
        total = combine(total, slot_a[k + 1])
    slot_b[0] = total
    copies = []
    for k in range(1, gy):
        copy = pltpu.make_async_remote_copy(
            src_ref=slot_b.at[0],
            dst_ref=slot_b.at[k],
            send_sem=send_b.at[k],
            recv_sem=recv_b.at[k],
            device_id=(mx, lax.rem(my + k, gy)),
            device_id_type=MESH,
        )
        copy.start()
        copies.append(copy)
    for k, copy in enumerate(copies):
        copy.wait()
        total = combine(total, slot_b[k + 1])
    out_ref[...] = total


def reduce_scalars(requests, top, gx, gy):
    count = requests.shape[0]
    tile = jnp.zeros((8, 128), jnp.float32)
    tile = tile.at[0, :].set(top).at[1, :count].set(requests)
    out = pl.pallas_call(
        lambda *refs: scalar_kernel(gx, gy, *refs),
        out_shape=jax.ShapeDtypeStruct((8, 128), jnp.float32),
        in_specs=[pl.BlockSpec(memory_space=pltpu.VMEM)],
        out_specs=pl.BlockSpec(memory_space=pltpu.VMEM),
        scratch_shapes=[
            pltpu.VMEM((gx, 8, 128), jnp.float32),
            pltpu.VMEM((gy, 8, 128), jnp.float32),
            pltpu.SemaphoreType.DMA((gx,)),
            pltpu.SemaphoreType.DMA((gx,)),
            pltpu.SemaphoreType.DMA((gy,)),
            pltpu.SemaphoreType.DMA((gy,)),
        ],
        compiler_params=pltpu.CompilerParams(collective_id=0, has_side_effects=True),
        name="scalar_sums",
    )(tile)
    return out[1, :count], out[0, 0]


def attend(projected, segment_ids):
    scores = jnp.einsum(
        "qhe,khe->hqk", projected[:, 0], projected[:, 1], preferred_element_type=jnp.float32
    ) / math.sqrt(HEAD)
    allowed = segment_ids[:, None] == segment_ids[None, :]
    scores = jnp.where(allowed[None], scores, -1e30)
    probs = jax.nn.softmax(scores, axis=-1).astype(jnp.bfloat16)
    mixed = jnp.einsum("hqk,khe->qhe", probs, projected[:, 2], preferred_element_type=jnp.float32)
    return mixed.astype(jnp.bfloat16)


def per_device(
    gx,
    gy,
    patches,
    segment_ids,
    image_requests,
    merge_index,
    qkv_weight,
    out_weight,
    up_weight,
    down_weight,
    merge_weight,
):
    tok_rows, feat_share = patches.shape
    group_index = lax.axis_index("gy")
    own_index = lax.axis_index("gx")
    ring = Ring(gy)
    head_share = qkv_weight.shape[2]
    local_heads = head_share // HEAD

    qkv_found = ring.gather(qkv_weight.reshape(qkv_weight.shape[0], -1), 1)
    up_found = ring.steps(up_weight)
    down_found = ring.gather(down_weight.T, 1)
    first_steps = step_of(up_found, 1) + step_of(down_found, 1)
    second_steps = step_of(up_found, 2) + step_of(down_found, 2)
    out_found = ring.gather(after(out_weight.T, *first_steps), 1)
    merge_full = lax.all_gather(after(merge_weight, *first_steps), "gy", axis=0, tiled=True)

    stream_full = gather_features(patches, gx)
    normed = layer_norm(stream_full.astype(jnp.float32)).astype(jnp.bfloat16)
    projected = sum_chunks(chunked(normed, gy), qkv_found)
    projected = after(projected.astype(jnp.bfloat16), *first_steps).reshape(tok_rows, 3, local_heads, HEAD)
    mixed = attend(projected, segment_ids).reshape(tok_rows, head_share)
    mixed = after(mixed, *second_steps)
    head_partial = place_columns(mixed, out_found, gy)
    stream_full = add_sum(head_partial, stream_full, gx)
    normed_two = layer_norm(stream_full.astype(jnp.float32)).astype(jnp.bfloat16)
    left = chunked(normed_two, gy)
    hidden = sum_chunks(left, up_found[:-2])
    cw, ccw, hidden = lax.optimization_barrier((up_found[-2][1], up_found[-1][1], hidden))
    ends = [(up_found[-2][0], cw), (up_found[-1][0], ccw), ring.last(cw, ccw, 1)]
    for index, shard in ends:
        hidden = add_chunk(left, hidden, index, shard)
    hidden = jax.nn.gelu(hidden, approximate=False).astype(jnp.bfloat16)
    unit_partial = place_columns(hidden, down_found, gy)
    final_full = add_sum(unit_partial, stream_full, gx)
    final_share = lax.dynamic_slice_in_dim(final_full, own_index * feat_share, feat_share, 1)
    row_squares = jnp.sum(jnp.square(final_share.astype(jnp.float32)), axis=1)
    image_ids = group_index * IMG_GRP + jnp.arange(IMG_GRP, dtype=jnp.int32)
    member = segment_ids[:, None] == image_ids[None, :]
    image_sq = jnp.sum(jnp.where(member, row_squares[:, None], 0.0), axis=0)
    local_requests = lax.dynamic_slice_in_dim(image_requests, group_index * IMG_GRP, IMG_GRP)
    request_count = image_requests.shape[0] // 4
    owner = local_requests[:, None] == jnp.arange(request_count, dtype=jnp.int32)[None, :]
    request_part = jnp.sum(jnp.where(owner, image_sq[:, None], 0.0), axis=0)
    local_index = (merge_index - group_index * tok_rows).reshape(-1)
    joined = jnp.take(final_full, local_index, axis=0).reshape(
        merge_index.shape[0], 4 * final_full.shape[1]
    )
    logits = jnp.dot(joined, merge_full, preferred_element_type=jnp.float32)
    local_top = jnp.max(logits)
    request_sq, top_logit = reduce_scalars(request_part, local_top, gx, gy)
    return (logits.astype(jnp.bfloat16), jnp.sqrt(request_sq), top_logit)


def solution(mesh):
    gx, gy = mesh.shape["gx"], mesh.shape["gy"]
    in_specs = (
        P("gy", "gx"),
        P("gy"),
        P(),
        P("gy", None),
        P("gy", None, "gx"),
        P("gx", "gy"),
        P("gy", "gx"),
        P("gx", "gy"),
        P("gy", "gx"),
    )
    out_specs = (P("gy", "gx"), P(), P())

    def body(*args):
        return per_device(gx, gy, *args)

    return jax.shard_map(
        body, mesh=mesh, in_specs=in_specs, out_specs=out_specs, check_vma=False
    )
```
